32 devices in a mesh: dp: 8 (over z, x), tensor: 4 (over y, core).
Axes of the slice: x: 2, y: 2, z: 4, core: 2. Of those that a mesh axis runs over, the one named last changes fastest.
Arguments:
- tokens: bfloat16 [8192, 2048], P(('dp', 'tensor')), may hold values from -6 to 6
- cotangent: bfloat16 [8192, 2048], P(('dp', 'tensor')), may hold values from -6 to 6
- norm1_gain: float32 [2048], replicated, may hold values from 0.5 to 1.5
- norm1_shift: float32 [2048], replicated, may hold values from -3 to 3
- query_weight: bfloat16 [2048, 2048], P('dp', 'tensor'), may hold values from -2 to 2
- query_bias: float32 [2048], replicated, may hold values from -5 to 5
- keyval_weight: bfloat16 [2048, 256], P('dp'), may hold values from -0.125 to 0.125
- value_bias: float32 [128], replicated, may hold values from -3 to 3
- out_weight: bfloat16 [2048, 2048], P('tensor', 'dp'), may hold values from -1.5 to 1.5
- out_bias: float32 [2048], replicated, may hold values from -3 to 3
- norm2_gain: float32 [2048], replicated, may hold values from 0.5 to 1.5
- norm2_shift: float32 [2048], replicated, may hold values from -3 to 3
- fc_weight: bfloat16 [2048, 8192], P('dp', 'tensor'), may hold values from -0.125 to 0.125
- fc_bias: float32 [8192], replicated, may hold values from -3 to 3
- proj_weight: bfloat16 [8192, 2048], P('tensor', 'dp'), may hold values from -0.0625 to 0.0625
- proj_bias: float32 [2048], replicated, may hold values from -3 to 3
Outputs:
- mixed: bfloat16 [8192, 2048], P(('dp', 'tensor'))
- token_grad: bfloat16 [8192, 2048], P(('dp', 'tensor'))
- norm1_gain_grad: float32 [2048], replicated
- norm1_shift_grad: float32 [2048], replicated
- query_weight_grad: float32 [2048, 2048], P('dp', 'tensor')
- query_bias_grad: float32 [2048], replicated
- keyval_weight_grad: float32 [2048, 256], P('dp')
- value_bias_grad: float32 [128], replicated
- out_weight_grad: float32 [2048, 2048], P('tensor', 'dp')
- out_bias_grad: float32 [2048], replicated
- norm2_gain_grad: float32 [2048], replicated
- norm2_shift_grad: float32 [2048], replicated
- fc_weight_grad: float32 [2048, 8192], P('dp', 'tensor')
- fc_bias_grad: float32 [8192], replicated
- proj_weight_grad: float32 [8192, 2048], P('tensor', 'dp')
- proj_bias_grad: float32 [2048], replicated
- clipped_query: bfloat16 [2048, 2048], P('dp', 'tensor')
- clipped_key: bfloat16 [2048, 128], P('dp')
The draws below stay inside these ranges and needn't reach their ends.
All inputs are finite; a program needn't handle non-finite values.
Results may differ from the reference program's by a relative error of at most 0.02.
Values may be sent and summed in bfloat16 or wider, within the bound.
No kernel may reach another device: no remote copies, remote signals or barrier semaphores. Data moves between devices by JAX's collectives and lax.ppermute only.
A program may use at most 192 MiB of HBM per device.

```python
import jax
import jax.numpy as jnp
from jax import lax

D = 2048
HEADS = 16
HEAD_DIM = 128
FF = 8192
SEQ_LEN = 1024
BLOCK = 256
TOKENS = 8192


def head_scales(key):
    order = jax.random.permutation(jax.random.fold_in(key, 11), HEADS)
    return 0.2 * 8.0 ** (order.astype(jnp.float32) / (HEADS - 1))


def draw_query_weight(key, part):
    scales = jnp.repeat(head_scales(key), HEAD_DIM)
    inner = jax.random.fold_in(key, 12)
    base = jax.random.truncated_normal(inner, -6.0, 6.0, (D, D), jnp.float32)
    return (base * D ** (-0.5) * scales[None, :]).astype(jnp.bfloat16)


def draw_query_bias(key, part):
    scales = jnp.repeat(head_scales(key), HEAD_DIM)
    inner = jax.random.fold_in(key, 13)
    base = 0.5 * jax.random.truncated_normal(inner, -6.0, 6.0, (D,), jnp.float32)
    return (base * scales).astype(jnp.float32)


def level_of(rng, extent, pieces, low, high):
    def one(axis_at, blocks):
        heights = jax.random.uniform(jax.random.fold_in(jax.random.fold_in(rng, 6), axis_at), (blocks,), jnp.float32, low / len(pieces), high / len(pieces))
        return jnp.repeat(jnp.exp(heights), extent[axis_at] // blocks).reshape((-1,) + (1,) * (len(extent) - axis_at - 1))

    factor_of = one(*pieces[0])
    for cut in pieces[1:]:
        factor_of = factor_of * one(*cut)
    return factor_of


def scatter_about(rng, shape, deviation, reach, split=(), kind=jnp.bfloat16):
    loudness = level_of(rng, shape, split, -0.22, 0.18) if split else 1.0
    drawn = jax.random.normal(rng, shape, jnp.float32) * deviation * loudness
    return jnp.minimum(jnp.maximum(drawn, -reach), reach).astype(kind)


def setup_inputs(seed: int = 0) -> dict:
    keys = jax.random.split(jax.random.key(seed), 17)
    return {
        "tokens": scatter_about(keys[0], (TOKENS, D), 1.0, 6.0, ((0, 32),)),
        "cotangent": scatter_about(keys[1], (TOKENS, D), 1.0, 6.0, ((0, 32),)),
        "norm1_gain": jnp.clip(1.0 + 0.1 * jax.random.normal(keys[2], (D,), jnp.float32), 0.5, 1.5),
        "norm1_shift": scatter_about(keys[3], (D,), 0.5, 3.0, (), jnp.float32),
        "query_weight": draw_query_weight(jax.random.fold_in(keys[16], 71), 0),
        "query_bias": draw_query_bias(jax.random.fold_in(keys[16], 71), 0),
        "keyval_weight": scatter_about(keys[6], (D, 2 * HEAD_DIM), D ** -0.5, 0.125, ((0, 8),)),
        "value_bias": scatter_about(keys[7], (HEAD_DIM,), 0.5, 3.0, (), jnp.float32),
        "out_weight": scatter_about(keys[8], (D, D), (max(1, 8 * D // SEQ_LEN)) ** -0.5, 1.5, ((0, 4), (1, 8))),
        "out_bias": scatter_about(keys[9], (D,), 0.5, 3.0, (), jnp.float32),
        "norm2_gain": jnp.clip(1.0 + 0.1 * jax.random.normal(keys[10], (D,), jnp.float32), 0.5, 1.5),
        "norm2_shift": scatter_about(keys[11], (D,), 0.5, 3.0, (), jnp.float32),
        "fc_weight": scatter_about(keys[12], (D, FF), D ** -0.5, 0.125, ((0, 8), (1, 4))),
        "fc_bias": scatter_about(keys[13], (FF,), 0.5, 3.0, (), jnp.float32),
        "proj_weight": scatter_about(keys[14], (FF, D), FF ** -0.5, 0.0625, ((0, 4), (1, 8))),
        "proj_bias": scatter_about(keys[15], (D,), 0.5, 3.0, (), jnp.float32),
    }


@jax.custom_vjp
def low(v):
    return lax.optimization_barrier(v.astype(jnp.bfloat16)).astype(jnp.float32)

@jax.custom_vjp
def low_back(v):
    return v

def low_keep(v):
    return (low(v), None)

def low_pass(kept, grad):
    return (grad,)

def back_keep(v):
    return (v, None)

def back_low(kept, grad):
    return (low(grad),)
low.defvjp(low_keep, low_pass)
low_back.defvjp(back_keep, back_low)
CLIP_LIMIT = 3.0

def matmul(first_operand, second_operand):
    return jnp.dot(first_operand, second_operand, precision=lax.Precision.HIGHEST)

def layer_norm(values, norm_gain, norm_shift):
    center = values - lax.optimization_barrier(jnp.mean(values, axis=-1, keepdims=True))
    spread = lax.optimization_barrier(jnp.mean(center * center, axis=-1, keepdims=True))
    return center * lax.rsqrt(spread + 1e-05) * norm_gain + norm_shift

def gelu_tanh(values):
    return 0.5 * values * (1.0 + jnp.tanh(0.7978845608028654 * (values + 0.044715 * values * values * values)))

def one_sequence(operands):
    queries, keyval = operands
    query_heads = queries.reshape(SEQ_LEN, HEADS, HEAD_DIM)
    key_rows = keyval[:, :HEAD_DIM]
    value_rows = keyval[:, HEAD_DIM:]
    scores = jnp.einsum('qhd,kd->hqk', query_heads, key_rows, precision=lax.Precision.HIGHEST) * HEAD_DIM ** (-0.5)
    scores = low_back(scores)
    blocks = jnp.arange(SEQ_LEN) // BLOCK
    allowed = blocks[None, :] <= blocks[:, None]
    masked = jnp.where(allowed[None], scores, -1e+30)
    largest = lax.optimization_barrier(jnp.max(masked, axis=(1, 2)))
    shifted = jnp.exp(masked - lax.optimization_barrier(jnp.max(masked, axis=-1, keepdims=True)))
    weights_soft = shifted / lax.optimization_barrier(jnp.sum(shifted, axis=-1, keepdims=True))
    attended = jnp.einsum('hqk,kd->qhd', low(weights_soft), value_rows, precision=lax.Precision.HIGHEST)
    return (attended.reshape(SEQ_LEN, HEADS * HEAD_DIM), largest)

def forward(params):
    tokens, norm1_gain, norm1_shift, query_weight, query_bias, keyval_weight, value_bias, out_weight, out_bias, norm2_gain, norm2_shift, fc_weight, fc_bias, proj_weight, proj_bias = params
    normed1 = low(layer_norm(tokens, norm1_gain, norm1_shift))
    queries = low(low_back(matmul(normed1, query_weight) + query_bias))
    kv_shift = jnp.concatenate([jnp.zeros((HEAD_DIM,), jnp.float32), value_bias])
    keyval = low(low_back(matmul(normed1, keyval_weight) + kv_shift))
    sequences = tokens.shape[0] // SEQ_LEN
    attended, largest = lax.map(jax.checkpoint(one_sequence), (queries.reshape(sequences, SEQ_LEN, D), keyval.reshape(sequences, SEQ_LEN, 2 * HEAD_DIM)))
    attended = low(low_back(attended.reshape(-1, D)))
    middle = tokens + low_back(matmul(attended, out_weight) + out_bias)
    normed2 = low(layer_norm(middle, norm2_gain, norm2_shift))
    hidden = low_back(matmul(normed2, fc_weight) + fc_bias)
    activated = low(gelu_tanh(hidden))
    result = middle + low_back(matmul(activated, proj_weight) + proj_bias)
    return (result, lax.optimization_barrier(jnp.max(largest, axis=0)))

def reference(tokens, cotangent, norm1_gain, norm1_shift, query_weight, query_bias, keyval_weight, value_bias, out_weight, out_bias, norm2_gain, norm2_shift, fc_weight, fc_bias, proj_weight, proj_bias):
    params = (tokens.astype(jnp.float32), norm1_gain.astype(jnp.float32), norm1_shift.astype(jnp.float32), query_weight.astype(jnp.float32), query_bias.astype(jnp.float32), keyval_weight.astype(jnp.float32), value_bias.astype(jnp.float32), out_weight.astype(jnp.float32), out_bias.astype(jnp.float32), norm2_gain.astype(jnp.float32), norm2_shift.astype(jnp.float32), fc_weight.astype(jnp.float32), fc_bias.astype(jnp.float32), proj_weight.astype(jnp.float32), proj_bias.astype(jnp.float32))
    result, pullback, peaks = jax.vjp(forward, params, has_aux=True)
    grads = pullback(cotangent.astype(jnp.float32))[0]
    clip_factor = CLIP_LIMIT / jnp.maximum(peaks, CLIP_LIMIT)
    key_factor = jnp.sqrt(jnp.min(clip_factor))
    column_factor = jnp.repeat(clip_factor / key_factor, HEAD_DIM)
    clipped_query = (params[3] * column_factor[None, :]).astype(jnp.bfloat16)
    clipped_key = (params[5][:, :HEAD_DIM] * key_factor).astype(jnp.bfloat16)
    return (result.astype(jnp.bfloat16), grads[0].astype(jnp.bfloat16), grads[1], grads[2], grads[3], grads[4], grads[5], grads[6], grads[7], grads[8], grads[9], grads[10], grads[11], grads[12], grads[13], grads[14], clipped_query, clipped_key)
```

```python
import jax
import jax.numpy as jnp
from jax import lax
from jax.sharding import PartitionSpec as P


HEADS = 16
HEAD_DIM = 128
SEQ_LEN = 1024
BLOCK = 256


CLIP_LIMIT = 3.0


def layer_norm(values, norm_gain, norm_shift):
    center = values - jnp.mean(values, axis=-1, keepdims=True)
    spread = jnp.mean(center * center, axis=-1, keepdims=True)
    return center * lax.rsqrt(spread + 1e-05) * norm_gain + norm_shift


def gelu_tanh(values):
    return (
        0.5
        * values
        * (1.0 + jnp.tanh(0.7978845608028654 * (values + 0.044715 * values * values * values)))
    )


def block_scores(query_block, key_rows, start, total):
    scores = jnp.einsum(
        "qhd,kd->hqk", query_block, key_rows, preferred_element_type=jnp.float32
    ) * HEAD_DIM ** (-0.5)
    query_pos = start + jnp.arange(query_block.shape[0])
    key_pos = jnp.arange(total)
    same_sequence = (query_pos // SEQ_LEN)[:, None] == (key_pos // SEQ_LEN)[None, :]
    earlier = (key_pos % SEQ_LEN // BLOCK)[None, :] <= (query_pos % SEQ_LEN // BLOCK)[:, None]
    return jnp.where((same_sequence & earlier)[None], scores, -1e30)


def attend_forward(queries, keyval, heads):
    total = queries.shape[0]
    rows_block = min(512, total)
    key_rows = keyval[:, :HEAD_DIM]
    value_rows = keyval[:, HEAD_DIM:]

    def one_block(start):
        query_block = lax.dynamic_slice_in_dim(queries, start, rows_block, 0).reshape(
            rows_block, heads, HEAD_DIM
        )
        masked = block_scores(query_block, key_rows, start, total)
        highest = jnp.max(masked, axis=-1, keepdims=True)
        shifted = jnp.exp(masked - highest)
        totals = jnp.sum(shifted, axis=-1, keepdims=True)
        weights_low = (shifted / totals).astype(jnp.bfloat16)
        attended = jnp.einsum(
            "hqk,kd->qhd", weights_low, value_rows, preferred_element_type=jnp.float32
        )
        logsum = highest[..., 0] + jnp.log(totals[..., 0])
        return (
            attended.reshape(rows_block, heads * HEAD_DIM).astype(jnp.bfloat16),
            logsum,
            jnp.max(highest[..., 0], axis=1),
        )

    starts = jnp.arange(total // rows_block, dtype=jnp.int32) * rows_block
    attended, logsums, peaks = lax.map(one_block, starts)
    return (attended.reshape(total, heads * HEAD_DIM), logsums, jnp.max(peaks, axis=0))


def attend_backward(queries, keyval, logsums, attended_grad, heads):
    total = queries.shape[0]
    rows_block = min(512, total)
    key_rows = keyval[:, :HEAD_DIM]
    value_rows = keyval[:, HEAD_DIM:]
    scale = HEAD_DIM ** (-0.5)

    def one_block(carry, operands):
        start, logsum = operands
        query_block = lax.dynamic_slice_in_dim(queries, start, rows_block, 0).reshape(
            rows_block, heads, HEAD_DIM
        )
        grad_block = lax.dynamic_slice_in_dim(attended_grad, start, rows_block, 0).reshape(
            rows_block, heads, HEAD_DIM
        )
        masked = block_scores(query_block, key_rows, start, total)
        weights_soft = jnp.exp(masked - logsum[..., None])
        weights_low = weights_soft.astype(jnp.bfloat16)
        weight_grad = jnp.einsum(
            "qhd,kd->hqk", grad_block, value_rows, preferred_element_type=jnp.float32
        )
        inner = jnp.sum(weights_soft * weight_grad, axis=-1, keepdims=True)
        score_grad = (weights_soft * (weight_grad - inner)).astype(jnp.bfloat16)
        query_grad = (
            jnp.einsum("hqk,kd->qhd", score_grad, key_rows, preferred_element_type=jnp.float32)
            * scale
        )
        key_grad = (
            carry[0]
            + jnp.einsum("hqk,qhd->kd", score_grad, query_block, preferred_element_type=jnp.float32)
            * scale
        )
        value_grad = carry[1] + jnp.einsum(
            "hqk,qhd->kd", weights_low, grad_block, preferred_element_type=jnp.float32
        )
        return (
            (key_grad, value_grad),
            query_grad.reshape(rows_block, heads * HEAD_DIM).astype(jnp.bfloat16),
        )

    starts = jnp.arange(total // rows_block, dtype=jnp.int32) * rows_block
    empty = jnp.zeros((total, HEAD_DIM), jnp.float32)
    (key_grad, value_grad), query_grad = lax.scan(one_block, (empty, empty), (starts, logsums))
    return (key_grad, value_grad, query_grad.reshape(total, heads * HEAD_DIM))


def dot_rows(first_operand, second_operand):
    return jnp.einsum(
        "ti,td->id", first_operand, second_operand, preferred_element_type=jnp.float32
    )


def dot_cols(first_operand, second_operand):
    return jnp.einsum(
        "ti,di->td", first_operand, second_operand, preferred_element_type=jnp.float32
    )


def dot(first_operand, second_operand):
    return jnp.dot(first_operand, second_operand, preferred_element_type=jnp.float32)


def low(values):
    return values.astype(jnp.bfloat16)


class Line:
    def __init__(self):
        self.size = lax.axis_size("dp")
        self.length = self.size // 2
        self.place = lax.axis_index("dp")

    def order(self, rank):
        far, step = divmod(rank, self.length)
        return self.place ^ (2 * step + far)

    def rank(self, block):
        offset = block ^ self.place
        return (offset % 2) * self.length + offset // 2

    def pick(self, values, blocks, axis):
        width = values.shape[axis] // self.size
        return jnp.concatenate(
            [lax.dynamic_slice_in_dim(values, block * width, width, axis) for block in blocks], axis
        )

    def inward(self, values, axis=-1):
        axis = axis % values.ndim
        return self.pick(values, [self.order(rank) for rank in range(self.size)], axis)

    def outward(self, values, axis=-1):
        axis = axis % values.ndim
        return self.pick(values, [self.rank(block) for block in range(self.size)], axis)

    def swap(self, values, offset):
        return lax.ppermute(values, "dp", [(i, i ^ offset) for i in range(self.size)])

    def gather_near(self, part):
        return [part] + [self.swap(part, 2 * step) for step in range(1, self.length)]

    def scatter(self, near, far, axis):
        total = near + self.swap(low(far), 1).astype(jnp.float32)
        pieces = jnp.split(total, self.length, axis)
        result = pieces[0]
        for step in range(1, self.length):
            result = result + self.swap(low(pieces[step]), 2 * step).astype(jnp.float32)
        return result


def halves(values, axis=1):
    return jnp.split(values, 2, axis)


def layer(
    tokens,
    cotangent,
    norm1_gain,
    norm1_shift,
    query_weight,
    query_bias,
    keyval_weight,
    value_bias,
    out_weight,
    out_bias,
    norm2_gain,
    norm2_shift,
    fc_weight,
    fc_bias,
    proj_weight,
    proj_bias,
):
    width = tokens.shape[1]
    split = lax.axis_size("tensor")
    position = lax.axis_index("tensor")
    line = Line()
    local_heads = HEADS // split
    query_cols = width // split
    hidden_all = fc_bias.shape[0]
    hidden_cols = hidden_all // split
    own_rows = tokens.shape[0]
    local_qbias = lax.dynamic_slice_in_dim(query_bias, position * query_cols, query_cols)
    local_fbias = lax.dynamic_slice_in_dim(fc_bias, position * hidden_cols, hidden_cols)

    attn_in = jnp.concatenate([query_weight, keyval_weight], axis=1)
    fc_parts, proj_parts = halves(fc_weight, 1), halves(proj_weight, 0)
    pieces_in = line.gather_near(attn_in)
    pieces_out = line.gather_near(out_weight)
    pieces_fc, pieces_proj = [], []
    for i in range(2):
        pieces_fc.append(line.gather_near(fc_parts[i]))
    for i in range(2):
        pieces_proj.append(line.gather_near(proj_parts[i]))
    in_near = jnp.concatenate(pieces_in, axis=0)
    in_far = line.swap(in_near, 1)
    out_near = jnp.concatenate(pieces_out, axis=1)
    out_far = line.swap(out_near, 1)
    fc_near, fc_far, proj_near, proj_far = [], [], [], []
    for i in range(2):
        fc_near.append(jnp.concatenate(pieces_fc[i], axis=0))
        fc_far.append(line.swap(fc_near[i], 1))
    for i in range(2):
        proj_near.append(jnp.concatenate(pieces_proj[i], axis=1))
        proj_far.append(line.swap(proj_near[i], 1))

    residual = line.inward(tokens).astype(jnp.float32)
    own_grad = line.inward(cotangent)
    gain1, shift1, gain2, shift2, bias_out, bias_proj = (
        line.inward(v)
        for v in (norm1_gain, norm1_shift, norm2_gain, norm2_shift, out_bias, proj_bias)
    )

    normed1 = lax.all_gather(
        low(layer_norm(residual, gain1, shift1)), "tensor", axis=0, tiled=True
    )
    out_grad = lax.all_gather(own_grad, "tensor", axis=0, tiled=True)
    normed1_near, normed1_far = halves(normed1)
    in_shift = jnp.concatenate([local_qbias, jnp.zeros((HEAD_DIM,), jnp.float32), value_bias])
    attn_all = low(dot(normed1_near, in_near) + dot(normed1_far, in_far) + in_shift)
    queries, keyval = attn_all[:, :query_cols], attn_all[:, query_cols:]
    attended, logsums, head_peaks = attend_forward(queries, keyval, local_heads)
    attn_terms = jnp.concatenate(
        [low(dot(attended, out_near)), low(dot(attended, out_far))], axis=1
    )
    middle = (
        residual
        + lax.psum_scatter(attn_terms, "tensor", scatter_dimension=0, tiled=True).astype(
            jnp.float32
        )
        + bias_out
    )
    normed2 = lax.all_gather(
        low(layer_norm(middle, gain2, shift2)), "tensor", axis=0, tiled=True
    )
    normed2_near, normed2_far = halves(normed2)
    out_grad_near, out_grad_far = halves(out_grad)

    fbias = halves(local_fbias, 0)
    hidden = []
    for i in range(2):
        hidden.append(
            dot(normed2_near, fc_near[i]) + dot(normed2_far, fc_far[i]) + fbias[i]
        )
    activated = [low(gelu_tanh(h)) for h in hidden]

    proj_sums, hidden_grad = [], []
    for i in range(2):
        proj_sums.append(
            line.scatter(
                dot_rows(activated[i], out_grad_near), dot_rows(activated[i], out_grad_far), 1
            )
        )
        activated_grad = dot_cols(out_grad_near, proj_near[i]) + dot_cols(
            out_grad_far, proj_far[i]
        )
        hidden_grad.append(low(jax.vjp(gelu_tanh, hidden[i])[1](activated_grad)[0]))
    normed2_terms = jnp.concatenate(
        [
            low(sum(dot_cols(hidden_grad[i], weights[i]) for i in range(2)))
            for weights in (fc_near, fc_far)
        ],
        axis=1,
    )
    normed2_grad = lax.psum_scatter(
        normed2_terms, "tensor", scatter_dimension=0, tiled=True
    ).astype(jnp.float32)
    fc_sums = [
        line.scatter(
            dot_rows(normed2_near, hidden_grad[i]), dot_rows(normed2_far, hidden_grad[i]), 0
        )
        for i in range(2)
    ]
    feed_terms = jnp.concatenate(
        [
            low(sum(dot(activated[i], weights[i]) for i in range(2)))
            for weights in (proj_near, proj_far)
        ],
        axis=1,
    )
    mixed = low(
        middle
        + lax.psum_scatter(feed_terms, "tensor", scatter_dimension=0, tiled=True).astype(
            jnp.float32
        )
        + bias_proj
    )

    middle_part, gain2_grad, shift2_grad = jax.vjp(layer_norm, middle, gain2, shift2)[1](
        normed2_grad
    )
    middle_grad = own_grad.astype(jnp.float32) + middle_part
    branch_grad = low(middle_grad)
    branch_rows = lax.all_gather(branch_grad, "tensor", axis=0, tiled=True)
    branch_near, branch_far = halves(branch_rows)
    attended_grad = low(dot_cols(branch_near, out_near) + dot_cols(branch_far, out_far))
    key_grad, value_grad, query_grad = attend_backward(
        queries, keyval, logsums, attended_grad, local_heads
    )
    out_sums = line.scatter(
        dot_rows(attended, branch_near), dot_rows(attended, branch_far), 1
    )
    keyval_grad = lax.psum(low(jnp.concatenate([key_grad, value_grad], axis=1)), "tensor")
    attn_grad = jnp.concatenate([query_grad, keyval_grad], axis=1)
    normed1_terms = jnp.concatenate(
        [
            low(dot_cols(query_grad, weights[:, :query_cols]))
            for weights in (in_near, in_far)
        ],
        axis=1,
    )
    in_sums = line.scatter(
        dot_rows(normed1_near, attn_grad), dot_rows(normed1_far, attn_grad), 0
    )
    keyval_own = lax.dynamic_slice_in_dim(keyval_grad, position * own_rows, own_rows, 0)
    normed1_grad = lax.psum_scatter(
        normed1_terms, "tensor", scatter_dimension=0, tiled=True
    ).astype(jnp.float32)
    normed1_grad = normed1_grad + jnp.concatenate(
        [dot_cols(keyval_own, weights[:, query_cols:]) for weights in (in_near, in_far)], axis=1
    )
    residual_part, gain1_grad, shift1_grad = jax.vjp(layer_norm, residual, gain1, shift1)[1](
        normed1_grad
    )
    token_grad = low(middle_grad + residual_part)

    count = line.size * split
    slots = lax.dynamic_update_slice_in_dim(
        jnp.zeros((count * local_heads,), jnp.float32),
        head_peaks,
        (line.place * split + position) * local_heads,
        0,
    )
    fc_bias_part = lax.dynamic_update_slice_in_dim(
        jnp.zeros((hidden_all,), jnp.float32),
        jnp.concatenate([jnp.sum(h, axis=0, dtype=jnp.float32) for h in hidden_grad]),
        position * hidden_cols,
        0,
    )
    early = [
        line.outward(gain2_grad),
        line.outward(shift2_grad),
        line.outward(jnp.sum(branch_grad, axis=0, dtype=jnp.float32)),
        line.outward(jnp.sum(own_grad, axis=0, dtype=jnp.float32)),
        fc_bias_part,
        slots,
    ]
    query_bias_part = lax.dynamic_update_slice_in_dim(
        jnp.zeros((width,), jnp.float32),
        jnp.sum(query_grad, axis=0, dtype=jnp.float32),
        position * query_cols,
        0,
    )
    late = [
        line.outward(gain1_grad),
        line.outward(shift1_grad),
        query_bias_part,
        jnp.sum(keyval_own[:, HEAD_DIM:], axis=0, dtype=jnp.float32),
    ]

    parts = early + late
    sizes = [part.shape[0] for part in parts]
    whole = jnp.concatenate(parts)
    moved = [
        lax.ppermute(whole, "tensor", [(i, i ^ step) for i in range(split)])
        for step in range(1, split)
    ]
    whole = sum(moved, whole)
    whole = whole + line.swap(whole, 1)
    moved = [line.swap(whole, 2 * step) for step in range(1, line.length)]
    whole = sum(moved, whole)
    ends = [sum(sizes[: i + 1]) for i in range(len(sizes) - 1)]
    (
        gain2_sum,
        shift2_sum,
        out_bias_sum,
        proj_bias_sum,
        fc_bias_sum,
        slot_sum,
        gain1_sum,
        shift1_sum,
        query_bias_sum,
        value_bias_sum,
    ) = jnp.split(whole, ends)

    peaks = jnp.max(slot_sum.reshape(line.size, HEADS), axis=0)
    clip_factor = CLIP_LIMIT / jnp.maximum(peaks, CLIP_LIMIT)
    key_factor = jnp.sqrt(jnp.min(clip_factor))
    local_clip = lax.dynamic_slice_in_dim(clip_factor, position * local_heads, local_heads)
    column_factor = jnp.repeat(local_clip / key_factor, HEAD_DIM)
    clipped_query = low(query_weight.astype(jnp.float32) * column_factor[None, :])
    clipped_key = low(keyval_weight[:, :HEAD_DIM].astype(jnp.float32) * key_factor)
    return (
        line.outward(mixed),
        line.outward(token_grad),
        gain1_sum,
        shift1_sum,
        in_sums[:, :query_cols],
        query_bias_sum,
        in_sums[:, query_cols:],
        value_bias_sum,
        out_sums,
        out_bias_sum,
        gain2_sum,
        shift2_sum,
        jnp.concatenate(fc_sums, axis=1),
        fc_bias_sum,
        jnp.concatenate(proj_sums, axis=0),
        proj_bias_sum,
        clipped_query,
        clipped_key,
    )


def solution(mesh):
    return jax.shard_map(
        layer,
        mesh=mesh,
        in_specs=(
            P(("dp", "tensor"), None),
            P(("dp", "tensor"), None),
            P(),
            P(),
            P("dp", "tensor"),
            P(),
            P("dp", None),
            P(),
            P("tensor", "dp"),
            P(),
            P(),
            P(),
            P("dp", "tensor"),
            P(),
            P("tensor", "dp"),
            P(),
        ),
        out_specs=(
            P(("dp", "tensor"), None),
            P(("dp", "tensor"), None),
            P(),
            P(),
            P("dp", "tensor"),
            P(),
            P("dp", None),
            P(),
            P("tensor", "dp"),
            P(),
            P(),
            P(),
            P("dp", "tensor"),
            P(),
            P("tensor", "dp"),
            P(),
            P("dp", "tensor"),
            P("dp", None),
        ),
        check_vma=False,
    )
```
